512 devices in a mesh: replica: 64 (over z_hi, y, x, core), tensor: 8 (over z_lo).
Axes of the slice: x: 4, y: 4, z: 16 (z_hi: 2, z_lo: 8; z = z_hi * 8 + z_lo), core: 2. Of those that a mesh axis runs over, the one named last changes fastest.
Arguments:
- tokens: bfloat16 [32768, 8192], P(('replica', 'tensor')), may hold values from -6 to 6
- norm_gain: bfloat16 [8192], replicated, may hold values from 0.099609375 to 1.8984375
- key_weight: bfloat16 [64, 8192, 1024], P('replica', None, 'tensor'), may hold values from -0.0625 to 0.0625
- inner_params: bfloat16 [64, 8, 1024, 512], P('replica', 'tensor'), may hold values from -16 to 16
- outer_params: float32 [8, 1024, 512], P('tensor', 'replica'), may hold values from -6 to 6
- outer_momentum: float32 [8, 1024, 512], P('tensor', 'replica'), may hold values from -3 to 3
Outputs:
- key_rows: bfloat16 [32768, 1024], P('replica', 'tensor')
- new_outer: float32 [8, 1024, 512], P('tensor', 'replica')
- new_momentum: float32 [8, 1024, 512], P('tensor', 'replica')
- synced_params: bfloat16 [8, 1024, 512], P('tensor')
The draws below stay inside these ranges and needn't reach their ends.
All inputs are finite; a program needn't handle non-finite values.
Results may differ from the reference program's by a relative error of at most 0.0049.
Values may be sent and summed in bfloat16 or wider, within the bound.
No kernel may reach another device: no remote copies, remote signals or barrier semaphores. Data moves between devices by JAX's collectives and lax.ppermute only.
A program may use at most 64 MiB of HBM per device.

```python
import math
import jax
import jax.numpy as jnp
from jax import lax

D = 8192
KVH = 8
HD = 128
TOK = 512
FRAG_ROWS = 1024
FRAG_COLS = 512
TOKENS = 32768
N_REPLICA = 64
N_TENSOR = 8


def strengthened(array, rng, source, target, shards_of, factor):
    def block_of(dim):
        return (jnp.arange(array.shape[dim]) // (array.shape[dim] // shards_of)).reshape((-1,) + (1,) * (array.ndim - 1 - dim))

    first = jax.random.permutation(rng, shards_of)[block_of(target)]
    other_side = (block_of(target) + shards_of // 2) % shards_of
    return jnp.where((block_of(source) == first) | (block_of(source) == other_side), factor * array, array)


def steps_of(own_key, shape, pieces, low, largest):
    gain = 1.0
    for axis_at, parts in pieces:
        heights = jax.random.uniform(jax.random.fold_in(jax.random.fold_in(own_key, 6), axis_at), (parts,), jnp.float32, low / len(pieces), largest / len(pieces))
        gain = gain * jnp.repeat(jnp.exp(heights), shape[axis_at] // parts).reshape((-1,) + (1,) * (len(shape) - 1 - axis_at))
    return gain


def centred(key, shape, width, limit, pieces=(), held_as=jnp.bfloat16):
    loudness = steps_of(key, shape, pieces, -0.22, 0.18) if pieces else 1.0
    result = jax.random.normal(key, shape, jnp.float32) * width * loudness
    return jnp.minimum(jnp.maximum(result, -limit), limit).astype(held_as)


def gaussian_with(key, extent, spread, limit, cuts, heavy, kind=jnp.bfloat16):
    entries = spread * jax.random.normal(key, extent, jnp.float32)
    if cuts:
        entries = entries * steps_of(key, extent, cuts, -0.22, 0.18)
    return jnp.clip(strengthened(entries, jax.random.fold_in(key, 3), *heavy), -limit, limit).astype(kind)


def setup_inputs(seed: int = 0) -> dict:
    key_of = jax.random.split(jax.random.key(seed), 7)
    return {
        "tokens": centred(key_of[0], (TOKENS, D), 1.0, 6.0, ((0, 512),)),
        "norm_gain": jnp.clip(1.0 + 0.18 * jax.random.normal(key_of[1], (D,), jnp.float32), 0.099609375, 1.8984375).astype(jnp.bfloat16),
        "key_weight": centred(key_of[2], (N_REPLICA, D, KVH * HD), D ** -0.5, 0.0625, ((0, 64), (2, 8))),
        "inner_params": gaussian_with(key_of[3], (N_REPLICA, N_TENSOR, FRAG_ROWS, FRAG_COLS), 1.0, 16.0, ((0, 64), (1, 8)), (0, 2, 64, 4.0)),
        "outer_params": centred(key_of[4], (N_TENSOR, FRAG_ROWS, FRAG_COLS), 1.0, 6.0, ((0, 8), (1, 64)), jnp.float32),
        "outer_momentum": centred(key_of[5], (N_TENSOR, FRAG_ROWS, FRAG_COLS), 0.5, 3.0, ((0, 8), (1, 64)), jnp.float32),
    }


EPSILON = 1e-05
ROPE_BASE = 500000.0
LR_OUTER = 0.7
MOMENTUM_OUTER = 0.9

def rotate(keys_f32, positions):
    rows = keys_f32.shape[0]
    cols = keys_f32.shape[1]
    half = HD // 2
    shaped = keys_f32.reshape(rows, cols // HD, HD)
    index = jnp.arange(half).astype(jnp.float32)
    inverse = jnp.exp(-(2.0 * index / HD) * math.log(ROPE_BASE))
    angles = positions[:, None] * inverse[None, :]
    cosine = jnp.cos(angles)[:, None, :]
    sine = jnp.sin(angles)[:, None, :]
    first = shaped[:, :, :half]
    second = shaped[:, :, half:]
    joined = jnp.concatenate([first * cosine - second * sine, second * cosine + first * sine], axis=-1)
    return joined.reshape(rows, cols)

def reference(tokens, norm_gain, key_weight, inner_params, outer_params, outer_momentum):
    gain_f32 = norm_gain.astype(jnp.float32)
    positions = jnp.arange(TOK).astype(jnp.float32)

    def forward_one(pair):
        block, weight = pair
        block_f32 = block.astype(jnp.float32)
        scale = lax.rsqrt(lax.optimization_barrier(jnp.mean(block_f32 * block_f32, axis=-1, keepdims=True)) + EPSILON)
        normed = (block_f32 * scale * gain_f32).astype(jnp.bfloat16)
        projected = jnp.dot(normed, weight, preferred_element_type=jnp.float32)
        return rotate(projected, positions).astype(jnp.bfloat16)
    blocks = tokens.reshape(N_REPLICA, TOK, D)
    key_rows = lax.map(forward_one, (blocks, key_weight)).reshape(N_REPLICA * TOK, KVH * HD)
    summed = lax.optimization_barrier(jnp.sum(inner_params, axis=0, dtype=jnp.float32))
    delta = outer_params - summed / N_REPLICA
    new_momentum = MOMENTUM_OUTER * outer_momentum + delta
    new_outer = outer_params - LR_OUTER * (delta + MOMENTUM_OUTER * new_momentum)
    synced_params = new_outer.astype(jnp.bfloat16)
    return (key_rows, new_outer, new_momentum, synced_params)
```

```python
import math

import jax
import jax.numpy as jnp
from jax import lax
from jax.sharding import Mesh
from jax.sharding import PartitionSpec as P

HD = 128


EPSILON = 1e-05
ROPE_BASE = 500000.0
LR_OUTER = 0.7
MOMENTUM_OUTER = 0.9

PLANE = ("y", "x", "core")
REPLICA = ("zh",) + PLANE


def rotate(keys_f32, positions):
    rows = keys_f32.shape[0]
    cols = keys_f32.shape[1]
    half = HD // 2
    shaped = keys_f32.reshape(rows, cols // HD, HD)
    index = jnp.arange(half).astype(jnp.float32)
    inverse = jnp.exp(-(2.0 * index / HD) * math.log(ROPE_BASE))
    angles = positions[:, None] * inverse[None, :]
    cosine = jnp.cos(angles)[:, None, :]
    sine = jnp.sin(angles)[:, None, :]
    first = shaped[:, :, :half]
    second = shaped[:, :, half:]
    joined = jnp.concatenate(
        [first * cosine - second * sine, second * cosine + first * sine], axis=-1
    )
    return joined.reshape(rows, cols)


def forward_keys(tokens, norm_gain, key_weight):
    block_f32 = tokens.astype(jnp.float32)
    scale = lax.rsqrt(jnp.mean(block_f32 * block_f32, axis=-1, keepdims=True) + EPSILON)
    normed = (block_f32 * scale * norm_gain.astype(jnp.float32)).astype(jnp.bfloat16)
    weight = key_weight[0]
    piece = lax.all_gather(normed, "tensor", axis=0, tiled=True)
    projected = jnp.dot(piece, weight, preferred_element_type=jnp.float32)
    positions = jnp.arange(piece.shape[0], dtype=jnp.int32).astype(jnp.float32)
    return rotate(projected, positions).astype(jnp.bfloat16)


def nesterov(outer_rows, moment_rows, summed, replicas):
    delta = outer_rows - summed / replicas
    moment_next = MOMENTUM_OUTER * moment_rows + delta
    outer_next = outer_rows - LR_OUTER * (delta + MOMENTUM_OUTER * moment_next)
    return (outer_next, moment_next)


def sync_fragment(inner_params, outer_params, outer_momentum):
    params = inner_params[0, 0].reshape(2, 32, 16, 512).transpose(1, 0, 2, 3)
    pieces = lax.all_to_all(params, PLANE, 0, 0, tiled=True)
    partial = jnp.sum(pieces.astype(jnp.float32), axis=0)
    zh = lax.axis_index("zh")
    other = lax.dynamic_index_in_dim(partial, 1 - zh, 0, keepdims=False)
    own = lax.dynamic_index_in_dim(partial, zh, 0, keepdims=False)
    summed = own + lax.ppermute(other, "zh", [(0, 1), (1, 0)])
    outer_next, moment_next = nesterov(outer_params[0], outer_momentum[0], summed, 64)
    mine = outer_next.astype(jnp.bfloat16)
    theirs = lax.ppermute(mine, "zh", [(0, 1), (1, 0)])
    pair = jnp.where(zh == 0, jnp.stack([mine, theirs]), jnp.stack([theirs, mine]))
    synced = lax.all_to_all(jnp.broadcast_to(pair[None], (32, 2, 16, 512)), PLANE, 0, 0, tiled=True)
    synced = synced.transpose(1, 0, 2, 3).reshape(1024, 512)
    return (outer_next[None], moment_next[None], synced[None])


def body(tokens, norm_gain, key_weight, inner_params, outer_params, outer_momentum):
    key_rows = forward_keys(tokens, norm_gain, key_weight)
    new_outer, new_momentum, synced_params = sync_fragment(
        inner_params, outer_params, outer_momentum
    )
    return (key_rows, new_outer, new_momentum, synced_params)


def solution(mesh):
    fine = Mesh(mesh.devices.reshape(2, 4, 4, 2, 8), REPLICA + ("tensor",))
    in_specs = (
        P(REPLICA + ("tensor",), None),
        P(),
        P(REPLICA, None, "tensor"),
        P(REPLICA, "tensor", None, None),
        P("tensor", REPLICA, None),
        P("tensor", REPLICA, None),
    )
    out_specs = (
        P(REPLICA, "tensor"),
        P("tensor", REPLICA, None),
        P("tensor", REPLICA, None),
        P("tensor", None, None),
    )
    return jax.shard_map(body, mesh=fine, in_specs=in_specs, out_specs=out_specs, check_vma=False)
```

```python
import math

import jax
import jax.numpy as jnp
from jax import lax
from jax.sharding import Mesh
from jax.sharding import PartitionSpec as P

HD = 128


EPSILON = 1e-05
ROPE_BASE = 500000.0
LR_OUTER = 0.7
MOMENTUM_OUTER = 0.9

PLANE = ("y", "x", "core")
REPLICA = ("zh",) + PLANE

K_LINE = 6144


def rotary_tables(rows):
    half = HD // 2
    index = jnp.arange(half).astype(jnp.float32)
    inverse = jnp.exp(-(2.0 * index / HD) * math.log(ROPE_BASE))
    angles = jnp.arange(rows).astype(jnp.float32)[:, None] * inverse[None, :]
    return jnp.cos(angles), jnp.sin(angles)


def dot(a, b):
    return jnp.dot(a, b, preferred_element_type=jnp.float32)


def after(mark, *values):
    return lax.optimization_barrier(values + (mark[:8, :128],))[: len(values)]


def nesterov(outer_rows, moment_rows, summed, replicas):
    delta = outer_rows - summed / replicas
    moment_next = MOMENTUM_OUTER * moment_rows + delta
    outer_next = outer_rows - LR_OUTER * (delta + MOMENTUM_OUTER * moment_next)
    return (outer_next, moment_next)


def body(tokens, norm_gain, key_weight, inner_params, outer_params, outer_momentum):
    me = lax.axis_index("tensor")
    zh = lax.axis_index("zh")
    low = me < 4
    params = inner_params[0, 0].reshape(2, 32, 16, 512).transpose(1, 0, 2, 3)
    pieces = lax.all_to_all(params, PLANE, 0, 0, tiled=True)

    block_f32 = tokens.astype(jnp.float32)
    scale = lax.rsqrt(jnp.mean(block_f32 * block_f32, axis=-1, keepdims=True) + EPSILON)
    normed = (block_f32 * scale * norm_gain.astype(jnp.float32)).astype(jnp.bfloat16)
    weight = key_weight[0]
    shard, rest = normed[:, :K_LINE], normed[:, K_LINE:]
    w_line, w_rest = weight[:K_LINE], weight[K_LINE:]

    rows = jnp.zeros((22, 64, HD), jnp.float32)

    def put(rows, block, at):
        return lax.dynamic_update_slice(rows, dot(block, w_line)[None], (7 + at, 0, 0))

    def hop(a, b, s):
        a = lax.ppermute(a, "tensor", [(j, j + 1) for j in range(s, 7)])
        b = lax.ppermute(b, "tensor", [(j + 1, j) for j in range(7 - s)])
        return a, b

    rows = put(rows, shard, me)
    a, b = hop(shard, shard, 0)
    rows = put(put(rows, a, me - 1), b, me + 1)

    (pieces,) = after(a, pieces)
    partial = jnp.sum(pieces.astype(jnp.float32), axis=0)
    other = lax.dynamic_index_in_dim(partial, 1 - zh, 0, keepdims=False)
    own = lax.dynamic_index_in_dim(partial, zh, 0, keepdims=False)
    came = lax.ppermute(other, "zh", [(0, 1), (1, 0)])

    a, b = hop(a, b, 1)
    rows = put(put(rows, a, me - 2), b, me + 2)

    (came,) = after(a, came)
    outer_next, moment_next = nesterov(outer_params[0], outer_momentum[0], own + came, 64)
    mine = outer_next.astype(jnp.bfloat16)
    theirs = lax.ppermute(mine, "zh", [(0, 1), (1, 0)])

    a, b = hop(a, b, 2)
    rows = put(put(rows, a, me - 3), b, me + 3)

    (theirs,) = after(a, theirs)
    pair = jnp.where(zh == 0, jnp.stack([mine, theirs]), jnp.stack([theirs, mine]))
    synced = lax.all_to_all(jnp.broadcast_to(pair[None], (32, 2, 16, 512)), PLANE, 0, 0, tiled=True)

    rest, w_rest = after(a, rest, w_rest)
    inward = {d: [(3 - d, 3), (4 + d, 4)] for d in (1, 2, 3)}
    held = [lax.ppermute(rest, "tensor", inward[d]) for d in (1, 2, 3)]
    wide = [lax.ppermute(w_rest, "tensor", inward[d]) for d in (1, 2, 3)]

    a, b = hop(a, b, 3)
    x = jnp.where(low, b, a)
    rows = put(rows, x, jnp.where(low, me + 4, me - 4))

    held = after(x, *held)
    near = jnp.concatenate((rest,) + tuple(held))
    far = lax.ppermute(near, "tensor", [(3, 4), (4, 3)])

    def hop_out(x, s):
        pairs = [(j, j + 1) for j in range(s, 7)] + [(j + 1, j) for j in range(7 - s)]
        return lax.ppermute(x, "tensor", pairs)

    x = hop_out(x, 4)
    rows = put(rows, x, jnp.where(low, me + 5, me - 5))
    x = hop_out(x, 5)
    rows = put(rows, x, jnp.where(low, me + 6, me - 6))

    far, synced, *wide = after(x, far, synced, *wide)
    synced = synced.transpose(1, 0, 2, 3).reshape(1024, 512)
    wide = jnp.concatenate([w_rest] + wide, axis=1)
    near, far = dot(near, wide), dot(far, wide)
    first = jnp.where(low, near, far).reshape(4, 64, 512)[::-1].reshape(256, 512)
    both = jnp.concatenate([first, jnp.where(low, far, near)])
    middle = jnp.where((me == 3) | (me == 4), both[:, :HD], 0.0)
    for d in (1, 2, 3):
        block = both[:, HD * d : HD * d + HD].astype(jnp.bfloat16)
        middle += lax.ppermute(block, "tensor", [(3, 3 - d), (4, 4 + d)]).astype(jnp.float32)

    x = hop_out(x, 6)
    rows = put(rows, x, jnp.where(low, me + 7, me - 7))
    projected = rows[7:15].reshape(512, HD) + middle
    cosine, sine = rotary_tables(512)
    first, second = projected[:, : HD // 2], projected[:, HD // 2 :]
    key_rows = jnp.concatenate(
        [first * cosine - second * sine, second * cosine + first * sine], axis=-1
    ).astype(jnp.bfloat16)
    return (key_rows, outer_next[None], moment_next[None], synced[None])


def solution(mesh):
    fine = Mesh(mesh.devices.reshape(2, 4, 4, 2, 8), REPLICA + ("tensor",))
    in_specs = (
        P(REPLICA + ("tensor",), None),
        P(),
        P(REPLICA, None, "tensor"),
        P(REPLICA, "tensor", None, None),
        P("tensor", REPLICA, None),
        P("tensor", REPLICA, None),
    )
    out_specs = (
        P(REPLICA, "tensor"),
        P("tensor", REPLICA, None),
        P("tensor", REPLICA, None),
        P("tensor", None, None),
    )
    return jax.shard_map(body, mesh=fine, in_specs=in_specs, out_specs=out_specs, check_vma=False)
```

```python
import math

import jax
import jax.numpy as jnp
from jax import lax
from jax.sharding import Mesh
from jax.sharding import PartitionSpec as P

HD = 128


EPSILON = 1e-05
ROPE_BASE = 500000.0
LR_OUTER = 0.7
MOMENTUM_OUTER = 0.9

PLANE = ("y", "x", "core")
REPLICA = ("zh",) + PLANE

K_LINE = 6144


def rotary_tables(rows):
    half = HD // 2
    index = jnp.arange(half).astype(jnp.float32)
    inverse = jnp.exp(-(2.0 * index / HD) * math.log(ROPE_BASE))
    angles = jnp.arange(rows).astype(jnp.float32)[:, None] * inverse[None, :]
    return jnp.cos(angles), jnp.sin(angles)


def dot(a, b):
    return jnp.dot(a, b, preferred_element_type=jnp.float32)


def after(mark, *values):
    return lax.optimization_barrier(values + (mark[:8, :128],))[: len(values)]


def nesterov(outer_rows, moment_rows, summed, replicas):
    delta = outer_rows - summed / replicas
    moment_next = MOMENTUM_OUTER * moment_rows + delta
    outer_next = outer_rows - LR_OUTER * (delta + MOMENTUM_OUTER * moment_next)
    return (outer_next, moment_next)


def body(tokens, norm_gain, key_weight, inner_params, outer_params, outer_momentum):
    me = lax.axis_index("tensor")
    zh = lax.axis_index("zh")
    low = me < 4
    params = inner_params[0, 0].reshape(2, 32, 16, 512).transpose(1, 0, 2, 3)
    pieces = lax.all_to_all(params, PLANE, 0, 0, tiled=True)

    block_f32 = tokens.astype(jnp.float32)
    scale = lax.rsqrt(jnp.mean(block_f32 * block_f32, axis=-1, keepdims=True) + EPSILON)
    normed = (block_f32 * scale * norm_gain.astype(jnp.float32)).astype(jnp.bfloat16)
    weight = key_weight[0]
    shard, rest = normed[:, :K_LINE], normed[:, K_LINE:]
    w_line, w_rest = weight[:K_LINE], weight[K_LINE:]

    rows = jnp.zeros((22, 64, HD), jnp.float32)

    def put(rows, block, at):
        return lax.dynamic_update_slice(rows, dot(block, w_line)[None], (7 + at, 0, 0))

    def hop(a, b, s):
        a = lax.ppermute(a, "tensor", [(j, j + 1) for j in range(s, 7)])
        b = lax.ppermute(b, "tensor", [(j + 1, j) for j in range(7 - s)])
        return a, b

    rows = put(rows, shard, me)
    a, b = hop(shard, shard, 0)
    rows = put(put(rows, a, me - 1), b, me + 1)

    (pieces,) = after(a, pieces)
    partial = jnp.sum(pieces.astype(jnp.float32), axis=0)
    other = lax.dynamic_index_in_dim(partial, 1 - zh, 0, keepdims=False)
    own = lax.dynamic_index_in_dim(partial, zh, 0, keepdims=False)
    came = lax.ppermute(other, "zh", [(0, 1), (1, 0)])

    a, b = hop(a, b, 1)
    rows = put(put(rows, a, me - 2), b, me + 2)

    (came,) = after(a, came)
    outer_next, moment_next = nesterov(outer_params[0], outer_momentum[0], own + came, 64)
    mine = outer_next.astype(jnp.bfloat16)
    theirs = lax.ppermute(mine, "zh", [(0, 1), (1, 0)])

    a, b = hop(a, b, 2)
    rows = put(put(rows, a, me - 3), b, me + 3)

    rows, rest, w_rest, theirs = lax.optimization_barrier((rows, rest, w_rest, theirs))
    inward = {d: [(3 - d, 3), (4 + d, 4)] for d in (1, 2, 3)}
    held = [lax.ppermute(rest, "tensor", inward[d]) for d in (1, 2, 3)]
    wide = [lax.ppermute(w_rest, "tensor", inward[d]) for d in (1, 2, 3)]

    a, b = hop(a, b, 3)
    x = jnp.where(low, b, a)
    x, *held = lax.optimization_barrier((x, *held))
    rows = put(rows, x, jnp.where(low, me + 4, me - 4))
    pair = jnp.where(zh == 0, jnp.stack([mine, theirs]), jnp.stack([theirs, mine]))
    near = jnp.concatenate((rest,) + tuple(held))
    far = lax.ppermute(near, "tensor", [(3, 4), (4, 3)])

    def hop_out(x, s):
        pairs = [(j, j + 1) for j in range(s, 7)] + [(j + 1, j) for j in range(7 - s)]
        return lax.ppermute(x, "tensor", pairs)

    synced = lax.all_to_all(jnp.broadcast_to(pair[None], (32, 2, 16, 512)), PLANE, 0, 0, tiled=True)

    x = hop_out(x, 4)
    rows = put(rows, x, jnp.where(low, me + 5, me - 5))
    x = hop_out(x, 5)
    rows = put(rows, x, jnp.where(low, me + 6, me - 6))

    rows, far, synced, *wide = lax.optimization_barrier((rows, far, synced, *wide))
    synced = synced.transpose(1, 0, 2, 3).reshape(1024, 512)
    wide = jnp.concatenate([w_rest] + wide, axis=1)
    near, far = dot(near, wide), dot(far, wide)
    first = jnp.where(low, near, far).reshape(4, 64, 512)[::-1].reshape(256, 512)
    both = jnp.concatenate([first, jnp.where(low, far, near)])
    middle = jnp.where((me == 3) | (me == 4), both[:, :HD], 0.0)
    for d in (1, 2, 3):
        block = both[:, HD * d : HD * d + HD].astype(jnp.bfloat16)
        middle += lax.ppermute(block, "tensor", [(3, 3 - d), (4, 4 + d)]).astype(jnp.float32)

    x = hop_out(x, 6)
    rows = put(rows, x, jnp.where(low, me + 7, me - 7))
    projected = rows[7:15].reshape(512, HD) + middle
    cosine, sine = rotary_tables(512)
    first, second = projected[:, : HD // 2], projected[:, HD // 2 :]
    key_rows = jnp.concatenate(
        [first * cosine - second * sine, second * cosine + first * sine], axis=-1
    ).astype(jnp.bfloat16)
    return (key_rows, outer_next[None], moment_next[None], synced[None])


def solution(mesh):
    fine = Mesh(mesh.devices.reshape(2, 4, 4, 2, 8), REPLICA + ("tensor",))
    in_specs = (
        P(REPLICA + ("tensor",), None),
        P(),
        P(REPLICA, None, "tensor"),
        P(REPLICA, "tensor", None, None),
        P("tensor", REPLICA, None),
        P("tensor", REPLICA, None),
    )
    out_specs = (
        P(REPLICA, "tensor"),
        P("tensor", REPLICA, None),
        P("tensor", REPLICA, None),
        P("tensor", None, None),
    )
    return jax.shard_map(body, mesh=fine, in_specs=in_specs, out_specs=out_specs, check_vma=False)
```

```python
import math

import jax
import jax.numpy as jnp
from jax import lax
from jax.sharding import Mesh
from jax.sharding import PartitionSpec as P

HD = 128


EPSILON = 1e-05
ROPE_BASE = 500000.0
LR_OUTER = 0.7
MOMENTUM_OUTER = 0.9

PLANE = ("y", "x", "core")
REPLICA = ("zh",) + PLANE

K_LINE = 5632


def rotary_tables(rows):
    half = HD // 2
    index = jnp.arange(half).astype(jnp.float32)
    inverse = jnp.exp(-(2.0 * index / HD) * math.log(ROPE_BASE))
    angles = jnp.arange(rows).astype(jnp.float32)[:, None] * inverse[None, :]
    return jnp.cos(angles), jnp.sin(angles)


def dot(a, b):
    return jnp.dot(a, b, preferred_element_type=jnp.float32)


def nesterov(outer_rows, moment_rows, summed, replicas):
    delta = outer_rows - summed / replicas
    moment_next = MOMENTUM_OUTER * moment_rows + delta
    outer_next = outer_rows - LR_OUTER * (delta + MOMENTUM_OUTER * moment_next)
    return (outer_next, moment_next)


def body(tokens, norm_gain, key_weight, inner_params, outer_params, outer_momentum):
    me = lax.axis_index("tensor")
    zh = lax.axis_index("zh")
    low = me < 4
    block_f32 = tokens.astype(jnp.float32)
    scale = lax.rsqrt(jnp.mean(block_f32 * block_f32, axis=-1, keepdims=True) + EPSILON)
    normed = (block_f32 * scale * norm_gain.astype(jnp.float32)).astype(jnp.bfloat16)
    weight = key_weight[0]
    shard, rest = normed[:, :K_LINE], normed[:, K_LINE:]
    w_line, w_rest = weight[:K_LINE], weight[K_LINE:]

    line = lax.all_gather(shard, "tensor", axis=0, tiled=True)

    inward = {d: [(3 - d, 3), (4 + d, 4)] for d in (1, 2, 3)}
    held = [lax.ppermute(rest, "tensor", inward[d]) for d in (1, 2, 3)]
    wide = [lax.ppermute(w_rest, "tensor", inward[d]) for d in (1, 2, 3)]
    near = jnp.concatenate([rest] + held)
    far = lax.ppermute(near, "tensor", [(3, 4), (4, 3)])
    wide = jnp.concatenate([w_rest] + wide, axis=1)
    near, far = dot(near, wide), dot(far, wide)
    first = jnp.where(low, near, far).reshape(4, 64, 512)[::-1].reshape(256, 512)
    both = jnp.concatenate([first, jnp.where(low, far, near)])
    middle = jnp.where((me == 3) | (me == 4), both[:, :HD], 0.0)
    for d in (1, 2, 3):
        block = both[:, HD * d : HD * d + HD].astype(jnp.bfloat16)
        middle += lax.ppermute(block, "tensor", [(3, 3 - d), (4, 4 + d)]).astype(jnp.float32)

    params = inner_params[0, 0].reshape(2, 32, 16, 512).transpose(1, 0, 2, 3)
    pieces = lax.all_to_all(params, PLANE, 0, 0, tiled=True)
    partial = jnp.sum(pieces.astype(jnp.float32), axis=0)
    other = lax.dynamic_index_in_dim(partial, 1 - zh, 0, keepdims=False)
    own = lax.dynamic_index_in_dim(partial, zh, 0, keepdims=False)
    came = lax.ppermute(other, "zh", [(0, 1), (1, 0)])
    outer_next, moment_next = nesterov(outer_params[0], outer_momentum[0], own + came, 64)
    mine = outer_next.astype(jnp.bfloat16)
    theirs = lax.ppermute(mine, "zh", [(0, 1), (1, 0)])
    pair = jnp.where(zh == 0, jnp.stack([mine, theirs]), jnp.stack([theirs, mine]))
    synced = lax.all_to_all(jnp.broadcast_to(pair[None], (32, 2, 16, 512)), PLANE, 0, 0, tiled=True)
    synced = synced.transpose(1, 0, 2, 3).reshape(1024, 512)

    projected = dot(line, w_line) + middle
    cosine, sine = rotary_tables(512)
    first, second = projected[:, : HD // 2], projected[:, HD // 2 :]
    key_rows = jnp.concatenate(
        [first * cosine - second * sine, second * cosine + first * sine], axis=-1
    ).astype(jnp.bfloat16)
    return (key_rows, outer_next[None], moment_next[None], synced[None])


def solution(mesh):
    fine = Mesh(mesh.devices.reshape(2, 4, 4, 2, 8), REPLICA + ("tensor",))
    in_specs = (
        P(REPLICA + ("tensor",), None),
        P(),
        P(REPLICA, None, "tensor"),
        P(REPLICA, "tensor", None, None),
        P("tensor", REPLICA, None),
        P("tensor", REPLICA, None),
    )
    out_specs = (
        P(REPLICA, "tensor"),
        P("tensor", REPLICA, None),
        P("tensor", REPLICA, None),
        P("tensor", None, None),
    )
    return jax.shard_map(body, mesh=fine, in_specs=in_specs, out_specs=out_specs, check_vma=False)
```

```python
import math

import jax
import jax.numpy as jnp
from jax import lax
from jax.sharding import Mesh
from jax.sharding import PartitionSpec as P

HD = 128


EPSILON = 1e-05
ROPE_BASE = 500000.0
LR_OUTER = 0.7
MOMENTUM_OUTER = 0.9

PLANE = ("y", "x", "core")
REPLICA = ("zh",) + PLANE

K_LINE = 6144


def rotary_tables(rows):
    half = HD // 2
    index = jnp.arange(half).astype(jnp.float32)
    inverse = jnp.exp(-(2.0 * index / HD) * math.log(ROPE_BASE))
    angles = jnp.arange(rows).astype(jnp.float32)[:, None] * inverse[None, :]
    return jnp.cos(angles), jnp.sin(angles)


def dot(a, b):
    return jnp.dot(a, b, preferred_element_type=jnp.float32)


def nesterov(outer_rows, moment_rows, summed, replicas):
    delta = outer_rows - summed / replicas
    moment_next = MOMENTUM_OUTER * moment_rows + delta
    outer_next = outer_rows - LR_OUTER * (delta + MOMENTUM_OUTER * moment_next)
    return (outer_next, moment_next)


hold = lax.optimization_barrier


def body(tokens, norm_gain, key_weight, inner_params, outer_params, outer_momentum):
    me = lax.axis_index("tensor")
    zh = lax.axis_index("zh")
    low = me < 4

    params = inner_params[0, 0].reshape(2, 32, 16, 512).transpose(1, 0, 2, 3)
    pieces = lax.all_to_all(params, PLANE, 0, 0, tiled=True)
    state = jnp.concatenate([outer_params, outer_momentum])
    state_other = lax.ppermute(state, "zh", [(0, 1), (1, 0)])

    block_f32 = tokens.astype(jnp.float32)
    scale = lax.rsqrt(jnp.mean(block_f32 * block_f32, axis=-1, keepdims=True) + EPSILON)
    normed = (block_f32 * scale * norm_gain.astype(jnp.float32)).astype(jnp.bfloat16)
    weight = key_weight[0]
    shard, rest = normed[:, :K_LINE], normed[:, K_LINE:]
    w_line, w_rest = weight[:K_LINE], weight[K_LINE:]

    rows = jnp.zeros((22, 64, HD), jnp.float32)

    def put(rows, block, at):
        return lax.dynamic_update_slice(rows, dot(block, w_line)[None], (7 + at, 0, 0))

    def hop(a, b, s):
        a = lax.ppermute(a, "tensor", [(j, j + 1) for j in range(s, 7)])
        b = lax.ppermute(b, "tensor", [(j + 1, j) for j in range(7 - s)])
        return a, b

    def hop_out(x, s):
        pairs = [(j, j + 1) for j in range(s, 7)] + [(j + 1, j) for j in range(7 - s)]
        return lax.ppermute(x, "tensor", pairs)

    def inward(x, d):
        return lax.ppermute(x, "tensor", [(3 - d, 4 - d), (4 + d, 3 + d)])

    a, b = hop(shard, shard, 0)
    rows = put(rows, shard, me)

    rows0 = put(put(rows, a, me - 1), b, me + 1)
    a, b = hop(a, b, 1)
    rows, pieces, state_other, rest, w_rest = hold((rows0, pieces, state_other, rest, w_rest))
    partial = jnp.sum(pieces.astype(jnp.float32), axis=0)
    came = lax.ppermute(partial, "zh", [(0, 1), (1, 0)])
    t3, w3 = inward(rest, 3), inward(w_rest, 3)

    rows1 = put(put(rows, a, me - 2), b, me + 2)
    a, b = hop(a, b, 2)
    rows, came, t3, w3 = hold((rows1, came, t3, w3))
    t2 = inward(jnp.concatenate([t3, rest]), 2)
    summed = partial + came
    ours = jnp.where(zh == 0, jnp.stack([state, state_other]), jnp.stack([state_other, state]))
    outer_pair, moment_pair = nesterov(ours[:, 0], ours[:, 1], summed, 64)
    outer_next = lax.dynamic_index_in_dim(outer_pair, zh, 0)
    moment_next = lax.dynamic_index_in_dim(moment_pair, zh, 0)
    pair = outer_pair.astype(jnp.bfloat16)

    rows2 = put(put(rows, a, me - 3), b, me + 3)
    a, b = hop(a, b, 3)
    rows, t2, w3 = hold((rows2, t2, w3))
    t1 = inward(jnp.concatenate([t2, rest]), 1)
    w3 = inward(w3, 2)

    x = jnp.where(low, b, a)
    rows3 = put(rows, x, jnp.where(low, me + 4, me - 4))
    x = hop_out(x, 4)
    rows, t1, w3, w2 = hold((rows3, t1, w3, w_rest))
    near = jnp.concatenate([t1, rest])
    far = lax.ppermute(near, "tensor", [(3, 4), (4, 3)])
    w13 = inward(jnp.concatenate([w_rest, w3]), 1)
    w2 = inward(w2, 2)

    rows4 = put(rows, x, jnp.where(low, me + 5, me - 5))
    x = hop_out(x, 5)
    rows, w2, pair = hold((rows4, w2, pair))
    w2 = inward(w2, 1)
    synced = lax.all_to_all(jnp.broadcast_to(pair[None], (32, 2, 16, 512)), PLANE, 0, 0, tiled=True)

    rows5 = put(rows, x, jnp.where(low, me + 6, me - 6))
    x = hop_out(x, 6)
    rows, far, w13, w2 = hold((rows5, far, w13, w2))
    size = w_rest.shape[0]
    wide = jnp.concatenate([w_rest, w13[:size], w2, w13[size:]], axis=1)
    near, far = dot(near, wide), dot(far, wide)
    last = jnp.where(low, far, near).reshape(4, 64, 512)[::-1].reshape(256, 512)
    both = jnp.concatenate([jnp.where(low, near, far), last])
    middle = jnp.where((me == 3) | (me == 4), both[:, :HD], 0.0)
    for d in (1, 2, 3):
        block = both[:, HD * d : HD * d + HD].astype(jnp.bfloat16)
        middle += lax.ppermute(block, "tensor", [(3, 3 - d), (4, 4 + d)]).astype(jnp.float32)

    rows = put(rows, x, jnp.where(low, me + 7, me - 7))
    synced = synced.transpose(1, 0, 2, 3).reshape(1024, 512)
    projected = rows[7:15].reshape(512, HD) + middle
    cosine, sine = rotary_tables(512)
    first, second = projected[:, : HD // 2], projected[:, HD // 2 :]
    key_rows = jnp.concatenate(
        [first * cosine - second * sine, second * cosine + first * sine], axis=-1
    ).astype(jnp.bfloat16)
    return (key_rows, outer_next, moment_next, synced[None])


def solution(mesh):
    fine = Mesh(mesh.devices.reshape(2, 4, 4, 2, 8), REPLICA + ("tensor",))
    in_specs = (
        P(REPLICA + ("tensor",), None),
        P(),
        P(REPLICA, None, "tensor"),
        P(REPLICA, "tensor", None, None),
        P("tensor", REPLICA, None),
        P("tensor", REPLICA, None),
    )
    out_specs = (
        P(REPLICA, "tensor"),
        P("tensor", REPLICA, None),
        P("tensor", REPLICA, None),
        P("tensor", None, None),
    )
    return jax.shard_map(body, mesh=fine, in_specs=in_specs, out_specs=out_specs, check_vma=False)
```

```python
import math

import jax
import jax.numpy as jnp
from jax import lax
from jax.experimental import pallas as pl
from jax.experimental.pallas import tpu as pltpu
from jax.sharding import Mesh
from jax.sharding import PartitionSpec as P

HD = 128


EPSILON = 1e-05
ROPE_BASE = 500000.0
LR_OUTER = 0.7
MOMENTUM_OUTER = 0.9

PLANE = ("y", "x", "core")
REPLICA = ("zh",) + PLANE

K_LINE = 5888


def rotary_tables(rows):
    half = HD // 2
    index = jnp.arange(half).astype(jnp.float32)
    inverse = jnp.exp(-(2.0 * index / HD) * math.log(ROPE_BASE))
    angles = jnp.arange(rows).astype(jnp.float32)[:, None] * inverse[None, :]
    return jnp.cos(angles), jnp.sin(angles)


def dot(a, b):
    return jnp.dot(a, b, preferred_element_type=jnp.float32)


def nesterov(outer_rows, moment_rows, summed, replicas):
    delta = outer_rows - summed / replicas
    moment_next = MOMENTUM_OUTER * moment_rows + delta
    outer_next = outer_rows - LR_OUTER * (delta + MOMENTUM_OUTER * moment_next)
    return (outer_next, moment_next)


hold = lax.optimization_barrier


def middle_kernel(low, near, far, w0, w13, w2, *outs):
    is_low = low[0] == 1
    size = w0.shape[0]
    w1, w3 = w13.at[:size], w13.at[size:]
    for pair, out in (((w0, w1), outs[:2]), ((w2, w3), outs[2:])):
        w = jnp.concatenate([pair[0][...], pair[1][...]], axis=1)
        p, q = dot(near[...], w), dot(far[...], w)
        first, last = jnp.where(is_low, p, q), jnp.where(is_low, q, p)
        for i, ref in enumerate(out):
            cols = slice(HD * i, HD * i + HD)
            ref[:256] = first[:, cols].astype(ref.dtype)
            for k in range(4):
                ref[256 + 64 * k : 320 + 64 * k] = last[192 - 64 * k : 256 - 64 * k, cols].astype(ref.dtype)


def middle_products(low, near, far, *weights):
    types = (jnp.float32, jnp.bfloat16, jnp.bfloat16, jnp.bfloat16)
    return pl.pallas_call(
        middle_kernel,
        out_shape=[jax.ShapeDtypeStruct((512, HD), t) for t in types],
        in_specs=[pl.BlockSpec(memory_space=pltpu.SMEM)] + [pl.BlockSpec(memory_space=pltpu.VMEM)] * 5,
        out_specs=[pl.BlockSpec(memory_space=pltpu.VMEM)] * 4,
        cost_estimate=pl.CostEstimate(flops=0, bytes_accessed=0, transcendentals=0),
        compiler_params=pltpu.CompilerParams(vmem_limit_bytes=24 << 20),
    )(low.astype(jnp.int32).reshape(1), near, far, *weights)


def body(tokens, norm_gain, key_weight, inner_params, outer_params, outer_momentum):
    me = lax.axis_index("tensor")
    zh = lax.axis_index("zh")
    low = me < 4

    params = inner_params[0, 0].reshape(2, 32, 16, 512).transpose(1, 0, 2, 3)
    pieces = lax.all_to_all(params, PLANE, 0, 0, tiled=True)

    gain = norm_gain.astype(jnp.float32)
    block_f32 = tokens.astype(jnp.float32)
    scale = lax.rsqrt(jnp.mean(block_f32 * block_f32, axis=-1, keepdims=True) + EPSILON)

    def normed(block, gain):
        return (block.astype(jnp.float32) * scale * gain).astype(jnp.bfloat16)

    weight = key_weight[0]
    w_line, w_rest = weight[:K_LINE], weight[K_LINE:]
    shard = normed(tokens[:, :K_LINE], gain[:K_LINE])

    rows = jnp.zeros((22, 64, HD), jnp.float32)

    def put(rows, block, at):
        return lax.dynamic_update_slice(rows, dot(block, w_line)[None], (7 + at, 0, 0))

    def hop(a, b, s):
        a = lax.ppermute(a, "tensor", [(j, j + 1) for j in range(s, 7)])
        b = lax.ppermute(b, "tensor", [(j + 1, j) for j in range(7 - s)])
        return a, b

    def hop_out(x, s):
        pairs = [(j, j + 1) for j in range(s, 7)] + [(j + 1, j) for j in range(7 - s)]
        return lax.ppermute(x, "tensor", pairs)

    def inward(x, d):
        return lax.ppermute(x, "tensor", [(3 - d, 4 - d), (4 + d, 3 + d)])

    a, b = hop(shard, shard, 0)
    rows = put(rows, shard, me)
    rows, rest_in = hold((rows, tokens[:, K_LINE:]))
    rest = normed(rest_in, gain[K_LINE:])

    rows0 = put(put(rows, a, me - 1), b, me + 1)
    a, b = hop(a, b, 1)
    rows, pieces, rest, w_rest = hold((rows0, pieces, rest, w_rest))
    t3, w3 = inward(rest, 3), inward(w_rest, 3)
    partial = jnp.sum(pieces.astype(jnp.float32), axis=0)
    other = lax.dynamic_index_in_dim(partial, 1 - zh, 0, keepdims=False)
    own = lax.dynamic_index_in_dim(partial, zh, 0, keepdims=False)
    came = lax.ppermute(other, "zh", [(0, 1), (1, 0)])

    rows1 = put(put(rows, a, me - 2), b, me + 2)
    a, b = hop(a, b, 2)
    rows, came, t3, w3 = hold((rows1, came, t3, w3))
    t2 = inward(jnp.concatenate([t3, rest]), 2)
    outer_next, moment_next = nesterov(outer_params[0], outer_momentum[0], own + came, 64)
    mine = outer_next.astype(jnp.bfloat16)
    theirs = lax.ppermute(mine, "zh", [(0, 1), (1, 0)])

    rows2 = put(put(rows, a, me - 3), b, me + 3)
    a, b = hop(a, b, 3)
    rows, t2, w3, theirs = hold((rows2, t2, w3, theirs))
    t1 = inward(jnp.concatenate([t2, rest]), 1)
    w3 = inward(w3, 2)
    pair = jnp.where(zh == 0, jnp.stack([mine, theirs]), jnp.stack([theirs, mine]))

    x = jnp.where(low, b, a)
    rows3 = put(rows, x, jnp.where(low, me + 4, me - 4))
    x = hop_out(x, 4)
    rows, t1, w3, w1, w2, pair = hold((rows3, t1, w3, w_rest, w_rest, pair))
    near = jnp.concatenate([t1, rest])
    far = lax.ppermute(near, "tensor", [(3, 4), (4, 3)])
    w13 = inward(jnp.concatenate([w1, w3]), 1)
    w2 = inward(w2, 2)

    rows4 = put(rows, x, jnp.where(low, me + 5, me - 5))
    x = hop_out(x, 5)
    rows, w2, w13, far = hold((rows4, w2, w13, far))
    w2 = inward(w2, 1)
    synced = lax.all_to_all(jnp.broadcast_to(pair[None], (32, 2, 16, 512)), PLANE, 0, 0, tiled=True)

    y = hop_out(x, 6)
    rows, w2, synced = hold((rows, w2, synced))
    rows5 = put(rows, x, jnp.where(low, me + 6, me - 6))
    rows, w2 = hold((rows5, w2))
    blocks = middle_products(low, near, far, w_rest, w13, w2)
    middle = jnp.where((me == 3) | (me == 4), blocks[0], 0.0)
    for d in (3, 2, 1):
        back = lax.ppermute(blocks[d], "tensor", [(3, 3 - d), (4, 4 + d)])
        middle += back.astype(jnp.float32)

    rows = put(rows, y, jnp.where(low, me + 7, me - 7))
    synced = synced.transpose(1, 0, 2, 3).reshape(1024, 512)
    projected = rows[7:15].reshape(512, HD) + middle
    cosine, sine = rotary_tables(512)
    first, second = projected[:, : HD // 2], projected[:, HD // 2 :]
    key_rows = jnp.concatenate(
        [first * cosine - second * sine, second * cosine + first * sine], axis=-1
    ).astype(jnp.bfloat16)
    return (key_rows, outer_next[None], moment_next[None], synced[None])


def solution(mesh):
    fine = Mesh(mesh.devices.reshape(2, 4, 4, 2, 8), REPLICA + ("tensor",))
    in_specs = (
        P(REPLICA + ("tensor",), None),
        P(),
        P(REPLICA, None, "tensor"),
        P(REPLICA, "tensor", None, None),
        P("tensor", REPLICA, None),
        P("tensor", REPLICA, None),
    )
    out_specs = (
        P(REPLICA, "tensor"),
        P("tensor", REPLICA, None),
        P("tensor", REPLICA, None),
        P("tensor", None, None),
    )
    return jax.shard_map(body, mesh=fine, in_specs=in_specs, out_specs=out_specs, check_vma=False)
```

```python
import math

import jax
import jax.numpy as jnp
from jax import lax
from jax.experimental import pallas as pl
from jax.experimental.pallas import tpu as pltpu
from jax.sharding import Mesh
from jax.sharding import PartitionSpec as P

HD = 128


EPSILON = 1e-05
ROPE_BASE = 500000.0
LR_OUTER = 0.7
MOMENTUM_OUTER = 0.9

PLANE = ("y", "x", "core")
REPLICA = ("zh",) + PLANE

K_LINE = 5888


def rotary_tables(rows):
    half = HD // 2
    index = jnp.arange(half).astype(jnp.float32)
    inverse = jnp.exp(-(2.0 * index / HD) * math.log(ROPE_BASE))
    angles = jnp.arange(rows).astype(jnp.float32)[:, None] * inverse[None, :]
    cosine, sine = jnp.cos(angles), jnp.sin(angles)
    return jnp.concatenate([cosine, cosine], axis=1), jnp.concatenate([-sine, sine], axis=1)


def dot(a, b):
    return jnp.dot(a, b, preferred_element_type=jnp.float32)


def nesterov(outer_rows, moment_rows, summed, replicas):
    delta = outer_rows - summed / replicas
    moment_next = MOMENTUM_OUTER * moment_rows + delta
    outer_next = outer_rows - LR_OUTER * (delta + MOMENTUM_OUTER * moment_next)
    return (outer_next, moment_next)


hold = lax.optimization_barrier


VMEM = pl.BlockSpec(memory_space=pltpu.VMEM)
SMEM = pl.BlockSpec(memory_space=pltpu.SMEM)
LINE = pl.BlockSpec((K_LINE, HD), lambda i: (0, 0))
FREE = dict(
    grid=(1,),
    cost_estimate=pl.CostEstimate(flops=0, bytes_accessed=0, transcendentals=0),
    compiler_params=pltpu.CompilerParams(vmem_limit_bytes=24 << 20),
)


def products_kernel(weight, *refs):
    n = len(refs) // 2
    both = dot(jnp.concatenate([block[...] for block in refs[:n]]), weight[...])
    for i, out in enumerate(refs[n:]):
        out[...] = both[64 * i : 64 * i + 64]


def products_cost(n):
    return pl.CostEstimate(flops=n * 2_000_000_000, bytes_accessed=0, transcendentals=0)


def products(weight, *blocks):
    return pl.pallas_call(
        products_kernel,
        out_shape=[jax.ShapeDtypeStruct((64, HD), jnp.float32)] * len(blocks),
        in_specs=[LINE] + [VMEM] * len(blocks),
        out_specs=[VMEM] * len(blocks),
        **dict(FREE, cost_estimate=products_cost(len(blocks))),
    )(weight, *blocks)


def last_kernel(at, weight, block, blocks, middle, back1, back2, back3, keep, turn, out, rows):
    for i in range(blocks.shape[0]):
        rows[pl.ds(pl.multiple_of(at[i] * 64, 64), 64)] = blocks[i]
    last = pl.multiple_of(at[blocks.shape[0]] * 64, 64)
    rows[pl.ds(last, 64)] = dot(block[...], weight[...])
    keys = rows[7 * 64 : 15 * 64] + jnp.where(at[blocks.shape[0] + 1] == 1, middle[...], 0.0)
    for back in (back1, back2, back3):
        keys += back[...].astype(jnp.float32)
    out[...] = (keys * keep[...] + pltpu.roll(keys, HD // 2, 1) * turn[...]).astype(out.dtype)


def last_step(at, weight, block, blocks, *rest):
    return pl.pallas_call(
        last_kernel,
        out_shape=jax.ShapeDtypeStruct((512, HD), jnp.bfloat16),
        in_specs=[SMEM, LINE] + [VMEM] * (2 + len(rest)),
        out_specs=VMEM,
        scratch_shapes=[pltpu.VMEM((22 * 64, HD), jnp.float32)],
        **FREE,
    )(at, weight, block, blocks, *rest)


def middle_kernel(low, near, far, w0, w13, w2, *outs):
    is_low = low[0] == 1
    size = w0.shape[0]
    w1, w3 = w13.at[:size], w13.at[size:]
    for pair, out in (((w0, w1), outs[:2]), ((w2, w3), outs[2:])):
        w = jnp.concatenate([pair[0][...], pair[1][...]], axis=1)
        p, q = dot(near[...], w), dot(far[...], w)
        first, last = jnp.where(is_low, p, q), jnp.where(is_low, q, p)
        for i, ref in enumerate(out):
            cols = slice(HD * i, HD * i + HD)
            ref[:256] = first[:, cols].astype(ref.dtype)
            for k in range(4):
                ref[256 + 64 * k : 320 + 64 * k] = last[192 - 64 * k : 256 - 64 * k, cols].astype(ref.dtype)


def middle_products(low, near, far, *weights):
    types = (jnp.float32, jnp.bfloat16, jnp.bfloat16, jnp.bfloat16)
    return pl.pallas_call(
        middle_kernel,
        out_shape=[jax.ShapeDtypeStruct((512, HD), t) for t in types],
        in_specs=[SMEM] + [VMEM] * 5,
        out_specs=[VMEM] * 4,
        **FREE,
    )(low.astype(jnp.int32).reshape(1), near, far, *weights)


def body(tokens, norm_gain, key_weight, inner_params, outer_params, outer_momentum):
    me = lax.axis_index("tensor")
    zh = lax.axis_index("zh")
    low = me < 4

    params = inner_params[0, 0].reshape(2, 32, 16, 512).transpose(1, 0, 2, 3)
    pieces = lax.all_to_all(params, PLANE, 0, 0, tiled=True)

    gain = norm_gain.astype(jnp.float32)
    block_f32 = tokens.astype(jnp.float32)
    scale = lax.rsqrt(jnp.mean(block_f32 * block_f32, axis=-1, keepdims=True) + EPSILON)

    def normed(block, gain):
        return (block.astype(jnp.float32) * scale * gain).astype(jnp.bfloat16)

    weight = key_weight[0]
    w_rest = weight[K_LINE:]
    shard = normed(tokens[:, :K_LINE], gain[:K_LINE])

    def hop(a, b, s):
        a = lax.ppermute(a, "tensor", [(j, j + 1) for j in range(s, 7)])
        b = lax.ppermute(b, "tensor", [(j + 1, j) for j in range(7 - s)])
        return a, b

    def hop_out(x, s):
        pairs = [(j, j + 1) for j in range(s, 7)] + [(j + 1, j) for j in range(7 - s)]
        return lax.ppermute(x, "tensor", pairs)

    def inward(x, d):
        return lax.ppermute(x, "tensor", [(3 - d, 4 - d), (4 + d, 3 + d)])

    a, b = hop(shard, shard, 0)
    (y,) = products(weight, shard)
    y, rest_in = hold((y, tokens[:, K_LINE:]))
    rest = normed(rest_in, gain[K_LINE:])

    y0 = products(weight, a, b)
    a, b = hop(a, b, 1)
    y0, pieces, rest, w_rest = hold((y0, pieces, rest, w_rest))
    t3, w3 = inward(rest, 3), inward(w_rest, 3)
    partial = jnp.sum(pieces.astype(jnp.float32), axis=0)
    other = lax.dynamic_index_in_dim(partial, 1 - zh, 0, keepdims=False)
    own = lax.dynamic_index_in_dim(partial, zh, 0, keepdims=False)
    came = lax.ppermute(other, "zh", [(0, 1), (1, 0)])

    y1 = products(weight, a, b)
    a, b = hop(a, b, 2)
    y1, came, t3, w3 = hold((y1, came, t3, w3))
    t2 = inward(jnp.concatenate([t3, rest]), 2)
    outer_next, moment_next = nesterov(outer_params[0], outer_momentum[0], own + came, 64)
    mine = outer_next.astype(jnp.bfloat16)
    theirs = lax.ppermute(mine, "zh", [(0, 1), (1, 0)])

    y2 = products(weight, a, b)
    a, b = hop(a, b, 3)
    y2, t2, w3, theirs = hold((y2, t2, w3, theirs))
    t1 = inward(jnp.concatenate([t2, rest]), 1)
    w3 = inward(w3, 2)
    pair = jnp.where(zh == 0, jnp.stack([mine, theirs]), jnp.stack([theirs, mine]))

    x = jnp.where(low, b, a)
    (y3,) = products(weight, x)
    x = hop_out(x, 4)
    y3, t1, w3, w1, w2, pair = hold((y3, t1, w3, w_rest, w_rest, pair))
    near = jnp.concatenate([t1, rest])
    far = lax.ppermute(near, "tensor", [(3, 4), (4, 3)])
    w13 = inward(jnp.concatenate([w1, w3]), 1)
    w2 = inward(w2, 2)

    (y4,) = products(weight, x)
    x = hop_out(x, 5)
    y4, w2, w13, far = hold((y4, w2, w13, far))
    w2 = inward(w2, 1)
    synced = lax.all_to_all(jnp.broadcast_to(pair[None], (32, 2, 16, 512)), PLANE, 0, 0, tiled=True)

    x5, synced = hold((x, synced))
    (y5,) = products(weight, x5)
    x = hop_out(x, 6)
    blocks = middle_products(low, near, far, w_rest, w13, w2)
    backs = [lax.ppermute(blocks[d], "tensor", [(3, 3 - d), (4, 4 + d)]) for d in (1, 2, 3)]

    at = [me] + [me + d for d in (-1, 1, -2, 2, -3, 3)]
    at += [jnp.where(low, me + d, me - d) for d in (4, 5, 6, 7)]
    at = jnp.stack([7 + i for i in at] + [((me == 3) | (me == 4)).astype(jnp.int32)])
    done = jnp.stack([y, *y0, *y1, *y2, y3, y4, y5])
    synced = synced.transpose(1, 0, 2, 3).reshape(1024, 512)
    key_rows = last_step(at, weight, x, done, blocks[0], *backs, *rotary_tables(512))
    return (key_rows, outer_next[None], moment_next[None], synced[None])


def solution(mesh):
    fine = Mesh(mesh.devices.reshape(2, 4, 4, 2, 8), REPLICA + ("tensor",))
    in_specs = (
        P(REPLICA + ("tensor",), None),
        P(),
        P(REPLICA, None, "tensor"),
        P(REPLICA, "tensor", None, None),
        P("tensor", REPLICA, None),
        P("tensor", REPLICA, None),
    )
    out_specs = (
        P(REPLICA, "tensor"),
        P("tensor", REPLICA, None),
        P("tensor", REPLICA, None),
        P("tensor", None, None),
    )
    return jax.shard_map(body, mesh=fine, in_specs=in_specs, out_specs=out_specs, check_vma=False)
```

```python
import math

import jax
import jax.numpy as jnp
from jax import lax
from jax.experimental import pallas as pl
from jax.experimental.pallas import tpu as pltpu
from jax.sharding import Mesh
from jax.sharding import PartitionSpec as P

HD = 128


EPSILON = 1e-05
ROPE_BASE = 500000.0
LR_OUTER = 0.7
MOMENTUM_OUTER = 0.9

PLANE = ("y", "x", "core")
REPLICA = ("zh",) + PLANE

K_LINE = 5888


def rotary_tables(rows):
    half = HD // 2
    index = jnp.arange(half).astype(jnp.float32)
    inverse = jnp.exp(-(2.0 * index / HD) * math.log(ROPE_BASE))
    angles = jnp.arange(rows).astype(jnp.float32)[:, None] * inverse[None, :]
    cosine, sine = jnp.cos(angles), jnp.sin(angles)
    return jnp.concatenate([cosine, cosine], axis=1), jnp.concatenate([-sine, sine], axis=1)


def dot(a, b):
    return jnp.dot(a, b, preferred_element_type=jnp.float32)


def nesterov(outer_rows, moment_rows, summed, replicas):
    delta = outer_rows - summed / replicas
    moment_next = MOMENTUM_OUTER * moment_rows + delta
    outer_next = outer_rows - LR_OUTER * (delta + MOMENTUM_OUTER * moment_next)
    return (outer_next, moment_next)


hold = lax.optimization_barrier


VMEM = pl.BlockSpec(memory_space=pltpu.VMEM)
SMEM = pl.BlockSpec(memory_space=pltpu.SMEM)
LINE = pl.BlockSpec((K_LINE, HD), lambda i: (0, 0))
FREE = dict(
    grid=(1,),
    cost_estimate=pl.CostEstimate(flops=0, bytes_accessed=0, transcendentals=0),
    compiler_params=pltpu.CompilerParams(vmem_limit_bytes=24 << 20),
)


def products_kernel(weight, *refs):
    n = len(refs) // 2
    both = dot(jnp.concatenate([block[...] for block in refs[:n]]), weight[...])
    for i, out in enumerate(refs[n:]):
        out[...] = both[64 * i : 64 * i + 64]


def products_cost(n):
    return pl.CostEstimate(flops=n * 2_000_000_000, bytes_accessed=0, transcendentals=0)


def products(weight, *blocks):
    return pl.pallas_call(
        products_kernel,
        out_shape=[jax.ShapeDtypeStruct((64, HD), jnp.float32)] * len(blocks),
        in_specs=[LINE] + [VMEM] * len(blocks),
        out_specs=[VMEM] * len(blocks),
        **dict(FREE, cost_estimate=products_cost(len(blocks))),
    )(weight, *blocks)


def last_kernel(at, weight, block, *refs):
    n = len(refs) - 8
    blocks, (middle, back1, back2, back3, keep, turn, out, rows) = refs[:n], refs[n:]
    for i, ref in enumerate(blocks):
        rows[pl.ds(pl.multiple_of(at[i] * 64, 64), 64)] = ref[...]
    rows[pl.ds(pl.multiple_of(at[n] * 64, 64), 64)] = dot(block[...], weight[...])
    keys = rows[7 * 64 : 15 * 64] + jnp.where(at[n + 1] == 1, middle[...], 0.0)
    for back in (back1, back2, back3):
        keys += back[...].astype(jnp.float32)
    out[...] = (keys * keep[...] + pltpu.roll(keys, HD // 2, 1) * turn[...]).astype(out.dtype)


def last_step(at, weight, block, *rest):
    return pl.pallas_call(
        last_kernel,
        out_shape=jax.ShapeDtypeStruct((512, HD), jnp.bfloat16),
        in_specs=[SMEM, LINE] + [VMEM] * (1 + len(rest)),
        out_specs=VMEM,
        scratch_shapes=[pltpu.VMEM((22 * 64, HD), jnp.float32)],
        **FREE,
    )(at, weight, block, *rest)


def sum_kernel(zh, pieces, other, own):
    for out, half in ((other, 1 - zh[0]), (own, zh[0])):
        total = pieces[0, half].astype(jnp.float32)
        for i in range(1, pieces.shape[0]):
            total += pieces[i, half].astype(jnp.float32)
        out[...] = total


def sum_pieces(zh, pieces):
    return pl.pallas_call(
        sum_kernel,
        out_shape=[jax.ShapeDtypeStruct((16, 512), jnp.float32)] * 2,
        in_specs=[SMEM, VMEM],
        out_specs=[VMEM] * 2,
        **dict(FREE, cost_estimate=products_cost(2)),
    )(zh.reshape(1), pieces)


def update_kernel(outer, moment, own, came, outer_next, moment_next, rounded):
    summed = own[...] + came[...]
    new_outer, new_moment = nesterov(outer[0], moment[0], summed, 64)
    outer_next[0] = new_outer
    moment_next[0] = new_moment
    rounded[...] = new_outer.astype(rounded.dtype)


def update(outer, moment, own, came):
    shape = jax.ShapeDtypeStruct((1, 16, 512), jnp.float32)
    return pl.pallas_call(
        update_kernel,
        out_shape=[shape, shape, jax.ShapeDtypeStruct((16, 512), jnp.bfloat16)],
        in_specs=[VMEM] * 4,
        out_specs=[VMEM] * 3,
        **dict(FREE, cost_estimate=products_cost(2)),
    )(outer, moment, own, came)


def middle_kernel(low, near, far, w0, w13, w2, *outs):
    is_low = low[0] == 1
    size = w0.shape[0]
    w1, w3 = w13.at[:size], w13.at[size:]
    for pair, out in (((w0, w1), outs[:2]), ((w2, w3), outs[2:])):
        w = jnp.concatenate([pair[0][...], pair[1][...]], axis=1)
        p, q = dot(near[...], w), dot(far[...], w)
        first, last = jnp.where(is_low, p, q), jnp.where(is_low, q, p)
        for i, ref in enumerate(out):
            cols = slice(HD * i, HD * i + HD)
            ref[:256] = first[:, cols].astype(ref.dtype)
            for k in range(4):
                ref[256 + 64 * k : 320 + 64 * k] = last[192 - 64 * k : 256 - 64 * k, cols].astype(ref.dtype)


def middle_products(low, near, far, *weights):
    types = (jnp.float32, jnp.bfloat16, jnp.bfloat16, jnp.bfloat16)
    return pl.pallas_call(
        middle_kernel,
        out_shape=[jax.ShapeDtypeStruct((512, HD), t) for t in types],
        in_specs=[SMEM] + [VMEM] * 5,
        out_specs=[VMEM] * 4,
        **FREE,
    )(low.astype(jnp.int32).reshape(1), near, far, *weights)


def body(tokens, norm_gain, key_weight, inner_params, outer_params, outer_momentum):
    me = lax.axis_index("tensor")
    zh = lax.axis_index("zh")
    low = me < 4

    params = inner_params[0, 0].reshape(2, 32, 16, 512).transpose(1, 0, 2, 3)
    pieces = lax.all_to_all(params, PLANE, 0, 0, tiled=True)

    gain = norm_gain.astype(jnp.float32)
    block_f32 = tokens.astype(jnp.float32)
    scale = lax.rsqrt(jnp.mean(block_f32 * block_f32, axis=-1, keepdims=True) + EPSILON)

    def normed(block, gain):
        return (block.astype(jnp.float32) * scale * gain).astype(jnp.bfloat16)

    weight = key_weight[0]
    w_rest = weight[K_LINE:]
    shard = normed(tokens[:, :K_LINE], gain[:K_LINE])

    def hop(a, b, s):
        a = lax.ppermute(a, "tensor", [(j, j + 1) for j in range(s, 7)])
        b = lax.ppermute(b, "tensor", [(j + 1, j) for j in range(7 - s)])
        return a, b

    def hop_out(x, s):
        pairs = [(j, j + 1) for j in range(s, 7)] + [(j + 1, j) for j in range(7 - s)]
        return lax.ppermute(x, "tensor", pairs)

    def inward(x, d):
        return lax.ppermute(x, "tensor", [(3 - d, 4 - d), (4 + d, 3 + d)])

    a, b = hop(shard, shard, 0)
    (y,) = products(weight, shard)
    y, rest_in = hold((y, tokens[:, K_LINE:]))
    rest = normed(rest_in, gain[K_LINE:])

    y0 = products(weight, a, b)
    a, b = hop(a, b, 1)
    y0, rest, w_rest = hold((y0, rest, w_rest))
    t3, w3 = inward(rest, 3), inward(w_rest, 3)

    y1 = products(weight, a, b)
    a, b = hop(a, b, 2)
    y1, t3, w3 = hold((y1, t3, w3))
    t2 = inward(jnp.concatenate([t3, rest]), 2)

    y2 = products(weight, a, b)
    a, b = hop(a, b, 3)
    y2, t2, w3, pieces = hold((y2, t2, w3, pieces))
    t1 = inward(jnp.concatenate([t2, rest]), 1)
    w3 = inward(w3, 2)
    other, own = sum_pieces(zh, pieces)
    came = lax.ppermute(other, "zh", [(0, 1), (1, 0)])

    x = jnp.where(low, b, a)
    (y3,) = products(weight, x)
    x = hop_out(x, 4)
    y3, t1, w3, w1, w2, came = hold((y3, t1, w3, w_rest, w_rest, came))
    w13, t1 = hold((jnp.concatenate([w1, w3]), t1))
    w13 = inward(w13, 1)
    near = jnp.concatenate([t1, rest])
    far = lax.ppermute(near, "tensor", [(3, 4), (4, 3)])
    w2 = inward(w2, 2)
    outer_next, moment_next, mine = update(outer_params, outer_momentum, own, came)
    theirs = lax.ppermute(mine, "zh", [(0, 1), (1, 0)])

    x4, theirs = hold((x, theirs))
    (y4,) = products(weight, x4)
    x = hop_out(x, 5)
    pair = jnp.where(zh == 0, jnp.stack([mine, theirs]), jnp.stack([theirs, mine]))
    y4, w2, w13, far = hold((y4, w2, w13, far))
    w2 = inward(w2, 1)
    synced = lax.all_to_all(jnp.broadcast_to(pair[None], (32, 2, 16, 512)), PLANE, 0, 0, tiled=True)

    x5, synced = hold((x, synced))
    (y5,) = products(weight, x5)
    x = hop_out(x, 6)
    blocks = middle_products(low, near, far, w_rest, w13, w2)
    backs = [lax.ppermute(blocks[d], "tensor", [(3, 3 - d), (4, 4 + d)]) for d in (1, 2, 3)]

    at = [me] + [me + d for d in (-1, 1, -2, 2, -3, 3)]
    at += [jnp.where(low, me + d, me - d) for d in (4, 5, 6, 7)]
    at = jnp.stack([7 + i for i in at] + [((me == 3) | (me == 4)).astype(jnp.int32)])
    synced = synced.transpose(1, 0, 2, 3).reshape(1024, 512)
    key_rows = last_step(
        at, weight, x, y, *y0, *y1, *y2, y3, y4, y5, blocks[0], *backs, *rotary_tables(512)
    )
    return (key_rows, outer_next, moment_next, synced[None])


def solution(mesh):
    fine = Mesh(mesh.devices.reshape(2, 4, 4, 2, 8), REPLICA + ("tensor",))
    in_specs = (
        P(REPLICA + ("tensor",), None),
        P(),
        P(REPLICA, None, "tensor"),
        P(REPLICA, "tensor", None, None),
        P("tensor", REPLICA, None),
        P("tensor", REPLICA, None),
    )
    out_specs = (
        P(REPLICA, "tensor"),
        P("tensor", REPLICA, None),
        P("tensor", REPLICA, None),
        P("tensor", None, None),
    )
    return jax.shard_map(body, mesh=fine, in_specs=in_specs, out_specs=out_specs, check_vma=False)
```

```python
import math

import jax
import jax.numpy as jnp
from jax import lax
from jax.experimental import pallas as pl
from jax.experimental.pallas import tpu as pltpu
from jax.sharding import Mesh
from jax.sharding import PartitionSpec as P

HD = 128


EPSILON = 1e-05
ROPE_BASE = 500000.0
LR_OUTER = 0.7
MOMENTUM_OUTER = 0.9

PLANE = ("y", "x", "core")
REPLICA = ("zh",) + PLANE

K_LINE = 6144


def rotary_tables(rows):
    half = HD // 2
    index = jnp.arange(half).astype(jnp.float32)
    inverse = jnp.exp(-(2.0 * index / HD) * math.log(ROPE_BASE))
    angles = jnp.arange(rows).astype(jnp.float32)[:, None] * inverse[None, :]
    return jnp.cos(angles), jnp.sin(angles)


def dot(a, b):
    return jnp.dot(a, b, preferred_element_type=jnp.float32)


def nesterov(outer_rows, moment_rows, summed, replicas):
    delta = outer_rows - summed / replicas
    moment_next = MOMENTUM_OUTER * moment_rows + delta
    outer_next = outer_rows - LR_OUTER * (delta + MOMENTUM_OUTER * moment_next)
    return (outer_next, moment_next)


hold = lax.optimization_barrier


def middle_kernel(low, near, far, w0, w13, w2, *outs):
    is_low = low[0] == 1
    size = w0.shape[0]
    w1, w3 = w13.at[:size], w13.at[size:]
    for pair, out in (((w0, w1), outs[:2]), ((w2, w3), outs[2:])):
        w = jnp.concatenate([pair[0][...], pair[1][...]], axis=1)
        p, q = dot(near[...], w), dot(far[...], w)
        first, last = jnp.where(is_low, p, q), jnp.where(is_low, q, p)
        for i, ref in enumerate(out):
            cols = slice(HD * i, HD * i + HD)
            ref[:256] = first[:, cols].astype(ref.dtype)
            for k in range(4):
                ref[256 + 64 * k : 320 + 64 * k] = last[192 - 64 * k : 256 - 64 * k, cols].astype(ref.dtype)


def middle_products(low, near, far, *weights):
    types = (jnp.float32, jnp.bfloat16, jnp.bfloat16, jnp.bfloat16)
    return pl.pallas_call(
        middle_kernel,
        out_shape=[jax.ShapeDtypeStruct((512, HD), t) for t in types],
        in_specs=[pl.BlockSpec(memory_space=pltpu.SMEM)] + [pl.BlockSpec(memory_space=pltpu.VMEM)] * 5,
        out_specs=[pl.BlockSpec(memory_space=pltpu.VMEM)] * 4,
        cost_estimate=pl.CostEstimate(flops=0, bytes_accessed=0, transcendentals=0),
        compiler_params=pltpu.CompilerParams(vmem_limit_bytes=24 << 20),
    )(low.astype(jnp.int32).reshape(1), near, far, *weights)


def body(tokens, norm_gain, key_weight, inner_params, outer_params, outer_momentum):
    me = lax.axis_index("tensor")
    zh = lax.axis_index("zh")
    low = me < 4

    params = inner_params[0, 0].reshape(2, 32, 16, 512).transpose(1, 0, 2, 3)
    pieces = lax.all_to_all(params, PLANE, 0, 0, tiled=True)

    gain = norm_gain.astype(jnp.float32)
    block_f32 = tokens.astype(jnp.float32)
    scale = lax.rsqrt(jnp.mean(block_f32 * block_f32, axis=-1, keepdims=True) + EPSILON)

    def normed(block, gain):
        return (block.astype(jnp.float32) * scale * gain).astype(jnp.bfloat16)

    weight = key_weight[0]
    w_line, w_rest = weight[:K_LINE], weight[K_LINE:]
    shard = normed(tokens[:, :K_LINE], gain[:K_LINE])

    rows = jnp.zeros((22, 64, HD), jnp.float32)

    def put(rows, block, at):
        return lax.dynamic_update_slice(rows, dot(block, w_line)[None], (7 + at, 0, 0))

    def hop(a, b, s):
        a = lax.ppermute(a, "tensor", [(j, j + 1) for j in range(s, 7)])
        b = lax.ppermute(b, "tensor", [(j + 1, j) for j in range(7 - s)])
        return a, b

    def hop_out(x, s):
        pairs = [(j, j + 1) for j in range(s, 7)] + [(j + 1, j) for j in range(7 - s)]
        return lax.ppermute(x, "tensor", pairs)

    def inward(x, d):
        return lax.ppermute(x, "tensor", [(3 - d, 4 - d), (4 + d, 3 + d)])

    a, b = hop(shard, shard, 0)
    rows = put(rows, shard, me)
    rows, rest_in = hold((rows, tokens[:, K_LINE:]))
    rest = normed(rest_in, gain[K_LINE:])

    rows0 = put(put(rows, a, me - 1), b, me + 1)
    a, b = hop(a, b, 1)
    rows, pieces, rest, w_rest = hold((rows0, pieces, rest, w_rest))
    t3, w3 = inward(rest, 3), inward(w_rest, 3)
    partial = jnp.sum(pieces.astype(jnp.float32), axis=0)
    other = lax.dynamic_index_in_dim(partial, 1 - zh, 0, keepdims=False)
    own = lax.dynamic_index_in_dim(partial, zh, 0, keepdims=False)
    came = lax.ppermute(other, "zh", [(0, 1), (1, 0)])

    rows1 = put(put(rows, a, me - 2), b, me + 2)
    a, b = hop(a, b, 2)
    rows, came, t3, w3 = hold((rows1, came, t3, w3))
    t2 = inward(jnp.concatenate([t3, rest]), 2)
    outer_next, moment_next = nesterov(outer_params[0], outer_momentum[0], own + came, 64)
    mine = outer_next.astype(jnp.bfloat16)
    theirs = lax.ppermute(mine, "zh", [(0, 1), (1, 0)])

    rows2 = put(put(rows, a, me - 3), b, me + 3)
    a, b = hop(a, b, 3)
    rows, t2, w3, theirs = hold((rows2, t2, w3, theirs))
    t1 = inward(jnp.concatenate([t2, rest]), 1)
    w3 = inward(w3, 2)
    pair = jnp.where(zh == 0, jnp.stack([mine, theirs]), jnp.stack([theirs, mine]))

    x = jnp.where(low, b, a)
    rows3 = put(rows, x, jnp.where(low, me + 4, me - 4))
    x = hop_out(x, 4)
    rows, t1, w3, w1, w2, pair = hold((rows3, t1, w3, w_rest, w_rest, pair))
    near = jnp.concatenate([t1, rest])
    far = lax.ppermute(near, "tensor", [(3, 4), (4, 3)])
    w13 = inward(jnp.concatenate([w1, w3]), 1)
    w2 = inward(w2, 2)

    rows4 = put(rows, x, jnp.where(low, me + 5, me - 5))
    x = hop_out(x, 5)
    rows, w2, w13, far = hold((rows4, w2, w13, far))
    w2 = inward(w2, 1)
    synced = lax.all_to_all(jnp.broadcast_to(pair[None], (32, 2, 16, 512)), PLANE, 0, 0, tiled=True)

    y = hop_out(x, 6)
    rows, synced = hold((rows, synced))
    rows = put(rows, x, jnp.where(low, me + 6, me - 6))
    blocks = middle_products(low, near, far, w_rest, w13, w2)
    middle = jnp.where((me == 3) | (me == 4), blocks[0], 0.0)
    for d in (3, 2, 1):
        back = lax.ppermute(blocks[d], "tensor", [(3, 3 - d), (4, 4 + d)])
        middle += back.astype(jnp.float32)

    rows = put(rows, y, jnp.where(low, me + 7, me - 7))
    synced = synced.transpose(1, 0, 2, 3).reshape(1024, 512)
    projected = rows[7:15].reshape(512, HD) + middle
    cosine, sine = rotary_tables(512)
    first, second = projected[:, : HD // 2], projected[:, HD // 2 :]
    key_rows = jnp.concatenate(
        [first * cosine - second * sine, second * cosine + first * sine], axis=-1
    ).astype(jnp.bfloat16)
    return (key_rows, outer_next[None], moment_next[None], synced[None])


def solution(mesh):
    fine = Mesh(mesh.devices.reshape(2, 4, 4, 2, 8), REPLICA + ("tensor",))
    in_specs = (
        P(REPLICA + ("tensor",), None),
        P(),
        P(REPLICA, None, "tensor"),
        P(REPLICA, "tensor", None, None),
        P("tensor", REPLICA, None),
        P("tensor", REPLICA, None),
    )
    out_specs = (
        P(REPLICA, "tensor"),
        P("tensor", REPLICA, None),
        P("tensor", REPLICA, None),
        P("tensor", None, None),
    )
    return jax.shard_map(body, mesh=fine, in_specs=in_specs, out_specs=out_specs, check_vma=False)
```

```python
import math

import jax
import jax.numpy as jnp
from jax import lax
from jax.experimental import pallas as pl
from jax.experimental.pallas import tpu as pltpu
from jax.sharding import Mesh
from jax.sharding import PartitionSpec as P

HD = 128


EPSILON = 1e-05
ROPE_BASE = 500000.0
LR_OUTER = 0.7
MOMENTUM_OUTER = 0.9

PLANE = ("y", "x", "core")
REPLICA = ("zh",) + PLANE

K_LINE = 5888


def rotary_tables(rows):
    half = HD // 2
    index = jnp.arange(half).astype(jnp.float32)
    inverse = jnp.exp(-(2.0 * index / HD) * math.log(ROPE_BASE))
    angles = jnp.arange(rows).astype(jnp.float32)[:, None] * inverse[None, :]
    return jnp.cos(angles), jnp.sin(angles)


def dot(a, b):
    return jnp.dot(a, b, preferred_element_type=jnp.float32)


def nesterov(outer_rows, moment_rows, summed, replicas):
    delta = outer_rows - summed / replicas
    moment_next = MOMENTUM_OUTER * moment_rows + delta
    outer_next = outer_rows - LR_OUTER * (delta + MOMENTUM_OUTER * moment_next)
    return (outer_next, moment_next)


hold = lax.optimization_barrier


def middle_kernel(low, near, far, *refs):
    is_low = low[0] == 1
    n = len(refs) // 2
    size = near.shape[1]
    columns = [ref[i : i + size] for ref in refs[:n] for i in range(0, ref.shape[0], size)]
    outs = refs[n:] if n == 1 else refs[2:]
    w = jnp.concatenate(columns, axis=1)
    p, q = dot(near[...], w), dot(far[...], w)
    first, last = jnp.where(is_low, p, q), jnp.where(is_low, q, p)
    for i, ref in enumerate(outs):
        cols = slice(HD * i, HD * i + HD)
        ref[:256] = first[:, cols].astype(ref.dtype)
        for k in range(4):
            ref[256 + 64 * k : 320 + 64 * k] = last[192 - 64 * k : 256 - 64 * k, cols].astype(ref.dtype)


def middle_products(low, near, far, *weights):
    types = (jnp.bfloat16,) if len(weights) == 1 else (jnp.float32, jnp.bfloat16, jnp.bfloat16)
    return pl.pallas_call(
        middle_kernel,
        out_shape=[jax.ShapeDtypeStruct((512, HD), t) for t in types],
        in_specs=[pl.BlockSpec(memory_space=pltpu.SMEM)] + [pl.BlockSpec(memory_space=pltpu.VMEM)] * (2 + len(weights)),
        out_specs=[pl.BlockSpec(memory_space=pltpu.VMEM)] * len(types),
        cost_estimate=pl.CostEstimate(flops=0, bytes_accessed=0, transcendentals=0),
        compiler_params=pltpu.CompilerParams(vmem_limit_bytes=24 << 20),
    )(low.astype(jnp.int32).reshape(1), near, far, *weights)


def body(tokens, norm_gain, key_weight, inner_params, outer_params, outer_momentum):
    me = lax.axis_index("tensor")
    zh = lax.axis_index("zh")
    low = me < 4

    params = inner_params[0, 0].reshape(2, 32, 16, 512).transpose(1, 0, 2, 3)
    pieces = lax.all_to_all(params, PLANE, 0, 0, tiled=True)

    gain = norm_gain.astype(jnp.float32)
    block_f32 = tokens.astype(jnp.float32)
    scale = lax.rsqrt(jnp.mean(block_f32 * block_f32, axis=-1, keepdims=True) + EPSILON)

    def normed(block, gain):
        return (block.astype(jnp.float32) * scale * gain).astype(jnp.bfloat16)

    weight = key_weight[0]
    w_line, w_rest = weight[:K_LINE], weight[K_LINE:]
    shard = normed(tokens[:, :K_LINE], gain[:K_LINE])

    rows = jnp.zeros((22, 64, HD), jnp.float32)

    def put(rows, block, at):
        return lax.dynamic_update_slice(rows, dot(block, w_line)[None], (7 + at, 0, 0))

    def hop(a, b, s):
        a = lax.ppermute(a, "tensor", [(j, j + 1) for j in range(s, 7)])
        b = lax.ppermute(b, "tensor", [(j + 1, j) for j in range(7 - s)])
        return a, b

    def hop_out(x, s):
        pairs = [(j, j + 1) for j in range(s, 7)] + [(j + 1, j) for j in range(7 - s)]
        return lax.ppermute(x, "tensor", pairs)

    def inward(x, d):
        return lax.ppermute(x, "tensor", [(3 - d, 4 - d), (4 + d, 3 + d)])

    a, b = hop(shard, shard, 0)
    rows = put(rows, shard, me)
    rows, rest_in = hold((rows, tokens[:, K_LINE:]))
    rest = normed(rest_in, gain[K_LINE:])

    rows0 = put(put(rows, a, me - 1), b, me + 1)
    a, b = hop(a, b, 1)
    rows, pieces, rest, w_rest = hold((rows0, pieces, rest, w_rest))
    t3, w3 = inward(rest, 3), inward(w_rest, 3)
    partial = jnp.sum(pieces.astype(jnp.float32), axis=0)
    other = lax.dynamic_index_in_dim(partial, 1 - zh, 0, keepdims=False)
    own = lax.dynamic_index_in_dim(partial, zh, 0, keepdims=False)
    came = lax.ppermute(other, "zh", [(0, 1), (1, 0)])

    rows1 = put(put(rows, a, me - 2), b, me + 2)
    a, b = hop(a, b, 2)
    rows, came, t3, w3 = hold((rows1, came, t3, w3))
    t2 = inward(jnp.concatenate([t3, rest]), 2)
    outer_next, moment_next = nesterov(outer_params[0], outer_momentum[0], own + came, 64)
    mine = outer_next.astype(jnp.bfloat16)
    theirs = lax.ppermute(mine, "zh", [(0, 1), (1, 0)])

    rows2 = put(put(rows, a, me - 3), b, me + 3)
    a, b = hop(a, b, 3)
    rows, t2, w3, theirs = hold((rows2, t2, w3, theirs))
    t1 = inward(jnp.concatenate([t2, rest]), 1)
    w3 = inward(w3, 2)
    pair = jnp.where(zh == 0, jnp.stack([mine, theirs]), jnp.stack([theirs, mine]))

    x = jnp.where(low, b, a)
    rows3 = put(rows, x, jnp.where(low, me + 4, me - 4))
    x = hop_out(x, 4)
    rows, t1, w3, w1, w2, pair = hold((rows3, t1, w3, w_rest, w_rest, pair))
    near = jnp.concatenate([t1, rest])
    far = lax.ppermute(near, "tensor", [(3, 4), (4, 3)])
    w13 = inward(jnp.concatenate([w1, w3]), 1)
    w2 = inward(w2, 2)

    rows4 = put(rows, x, jnp.where(low, me + 5, me - 5))
    x = hop_out(x, 5)
    rows, w2, w13, far = hold((rows4, w2, w13, far))
    w2 = inward(w2, 1)
    synced = lax.all_to_all(jnp.broadcast_to(pair[None], (32, 2, 16, 512)), PLANE, 0, 0, tiled=True)

    y = hop_out(x, 6)
    rows, w2, synced = hold((rows, w2, synced))
    rows = put(rows, x, jnp.where(low, me + 6, me - 6))
    mine3, back1, back3 = middle_products(low, near, far, w_rest, w13)
    (back2,) = middle_products(low, near, far, w2)
    middle = jnp.where((me == 3) | (me == 4), mine3, 0.0)
    for d, block in ((3, back3), (1, back1), (2, back2)):
        back = lax.ppermute(block, "tensor", [(3, 3 - d), (4, 4 + d)])
        middle += back.astype(jnp.float32)

    rows = put(rows, y, jnp.where(low, me + 7, me - 7))
    synced = synced.transpose(1, 0, 2, 3).reshape(1024, 512)
    projected = rows[7:15].reshape(512, HD) + middle
    cosine, sine = rotary_tables(512)
    first, second = projected[:, : HD // 2], projected[:, HD // 2 :]
    key_rows = jnp.concatenate(
        [first * cosine - second * sine, second * cosine + first * sine], axis=-1
    ).astype(jnp.bfloat16)
    return (key_rows, outer_next[None], moment_next[None], synced[None])


def solution(mesh):
    fine = Mesh(mesh.devices.reshape(2, 4, 4, 2, 8), REPLICA + ("tensor",))
    in_specs = (
        P(REPLICA + ("tensor",), None),
        P(),
        P(REPLICA, None, "tensor"),
        P(REPLICA, "tensor", None, None),
        P("tensor", REPLICA, None),
        P("tensor", REPLICA, None),
    )
    out_specs = (
        P(REPLICA, "tensor"),
        P("tensor", REPLICA, None),
        P("tensor", REPLICA, None),
        P("tensor", None, None),
    )
    return jax.shard_map(body, mesh=fine, in_specs=in_specs, out_specs=out_specs, check_vma=False)
```

```python
import math

import jax
import jax.numpy as jnp
from jax import lax
from jax.experimental import pallas as pl
from jax.experimental.pallas import tpu as pltpu
from jax.sharding import Mesh
from jax.sharding import PartitionSpec as P

HD = 128


EPSILON = 1e-05
ROPE_BASE = 500000.0
LR_OUTER = 0.7
MOMENTUM_OUTER = 0.9

PLANE = ("y", "x", "core")
REPLICA = ("zh",) + PLANE

K_LINE = 5888


def rotary_tables(rows):
    half = HD // 2
    index = jnp.arange(half).astype(jnp.float32)
    inverse = jnp.exp(-(2.0 * index / HD) * math.log(ROPE_BASE))
    angles = jnp.arange(rows).astype(jnp.float32)[:, None] * inverse[None, :]
    cosine, sine = jnp.cos(angles), jnp.sin(angles)
    return jnp.concatenate([cosine, cosine], axis=1), jnp.concatenate([-sine, sine], axis=1)


def dot(a, b):
    return jnp.dot(a, b, preferred_element_type=jnp.float32)


def nesterov(outer_rows, moment_rows, summed, replicas):
    delta = outer_rows - summed / replicas
    moment_next = MOMENTUM_OUTER * moment_rows + delta
    outer_next = outer_rows - LR_OUTER * (delta + MOMENTUM_OUTER * moment_next)
    return (outer_next, moment_next)


hold = lax.optimization_barrier


def middle_kernel(low, near, far, *refs):
    is_low = low[0] == 1
    n = len(refs) // 2
    size = near.shape[1]
    columns = [ref[i : i + size] for ref in refs[:n] for i in range(0, ref.shape[0], size)]
    outs = refs[n:] if n == 1 else refs[2:]
    w = jnp.concatenate(columns, axis=1)
    p, q = dot(near[...], w), dot(far[...], w)
    first, last = jnp.where(is_low, p, q), jnp.where(is_low, q, p)
    for i, ref in enumerate(outs):
        cols = slice(HD * i, HD * i + HD)
        ref[:256] = first[:, cols].astype(ref.dtype)
        for k in range(4):
            ref[256 + 64 * k : 320 + 64 * k] = last[192 - 64 * k : 256 - 64 * k, cols].astype(ref.dtype)


def middle_products(low, near, far, *weights):
    types = (jnp.bfloat16,) if len(weights) == 1 else (jnp.float32, jnp.bfloat16, jnp.bfloat16)
    return pl.pallas_call(
        middle_kernel,
        out_shape=[jax.ShapeDtypeStruct((512, HD), t) for t in types],
        in_specs=[pl.BlockSpec(memory_space=pltpu.SMEM)] + [pl.BlockSpec(memory_space=pltpu.VMEM)] * (2 + len(weights)),
        out_specs=[pl.BlockSpec(memory_space=pltpu.VMEM)] * len(types),
        cost_estimate=pl.CostEstimate(flops=0, bytes_accessed=0, transcendentals=0),
        compiler_params=pltpu.CompilerParams(vmem_limit_bytes=24 << 20),
    )(low.astype(jnp.int32).reshape(1), near, far, *weights)


def last_kernel(me, weight, block, rows, mine, back1, back2, back3, keep, turn, out):
    at = me[0]
    last = dot(block[...], weight[...])
    keys = rows[7:15].reshape(512, HD) + jnp.where((at == 3) | (at == 4), mine[...], 0.0)
    for back in (back1, back2, back3):
        keys += back[...].astype(jnp.float32)
    head = keys[:64] + jnp.where(at == 7, last, 0.0)
    tail = keys[448:] + jnp.where(at == 0, last, 0.0)
    keys = jnp.concatenate([head, keys[64:448], tail])
    out[...] = (keys * keep[...] + pltpu.roll(keys, HD // 2, 1) * turn[...]).astype(out.dtype)


def last_step(me, weight, *rest):
    vmem = pl.BlockSpec(memory_space=pltpu.VMEM)
    return pl.pallas_call(
        last_kernel,
        grid=(1,),
        out_shape=jax.ShapeDtypeStruct((512, HD), jnp.bfloat16),
        in_specs=[pl.BlockSpec(memory_space=pltpu.SMEM), pl.BlockSpec((K_LINE, HD), lambda i: (0, 0))]
        + [vmem] * len(rest),
        out_specs=vmem,
        cost_estimate=pl.CostEstimate(flops=2 * 64 * K_LINE * HD, bytes_accessed=0, transcendentals=0),
        compiler_params=pltpu.CompilerParams(vmem_limit_bytes=24 << 20),
    )(me.reshape(1), weight, *rest)


def body(tokens, norm_gain, key_weight, inner_params, outer_params, outer_momentum):
    me = lax.axis_index("tensor")
    zh = lax.axis_index("zh")
    low = me < 4

    params = inner_params[0, 0].reshape(2, 32, 16, 512).transpose(1, 0, 2, 3)
    pieces = lax.all_to_all(params, PLANE, 0, 0, tiled=True)

    gain = norm_gain.astype(jnp.float32)
    block_f32 = tokens.astype(jnp.float32)
    scale = lax.rsqrt(jnp.mean(block_f32 * block_f32, axis=-1, keepdims=True) + EPSILON)

    def normed(block, gain):
        return (block.astype(jnp.float32) * scale * gain).astype(jnp.bfloat16)

    weight = key_weight[0]
    w_line, w_rest = weight[:K_LINE], weight[K_LINE:]
    shard = normed(tokens[:, :K_LINE], gain[:K_LINE])

    rows = jnp.zeros((22, 64, HD), jnp.float32)

    def put(rows, block, at):
        return lax.dynamic_update_slice(rows, dot(block, w_line)[None], (7 + at, 0, 0))

    def hop(a, b, s):
        a = lax.ppermute(a, "tensor", [(j, j + 1) for j in range(s, 7)])
        b = lax.ppermute(b, "tensor", [(j + 1, j) for j in range(7 - s)])
        return a, b

    def hop_out(x, s):
        pairs = [(j, j + 1) for j in range(s, 7)] + [(j + 1, j) for j in range(7 - s)]
        return lax.ppermute(x, "tensor", pairs)

    def inward(x, d):
        return lax.ppermute(x, "tensor", [(3 - d, 4 - d), (4 + d, 3 + d)])

    a, b = hop(shard, shard, 0)
    rows = put(rows, shard, me)
    rows, rest_in = hold((rows, tokens[:, K_LINE:]))
    rest = normed(rest_in, gain[K_LINE:])

    rows0 = put(put(rows, a, me - 1), b, me + 1)
    a, b = hop(a, b, 1)
    rows, pieces, rest, w_rest = hold((rows0, pieces, rest, w_rest))
    t3, w3 = inward(rest, 3), inward(w_rest, 3)
    partial = jnp.sum(pieces.astype(jnp.float32), axis=0)
    other = lax.dynamic_index_in_dim(partial, 1 - zh, 0, keepdims=False)
    own = lax.dynamic_index_in_dim(partial, zh, 0, keepdims=False)
    came = lax.ppermute(other, "zh", [(0, 1), (1, 0)])

    rows1 = put(put(rows, a, me - 2), b, me + 2)
    a, b = hop(a, b, 2)
    rows, came, t3, w3 = hold((rows1, came, t3, w3))
    t2 = inward(jnp.concatenate([t3, rest]), 2)
    outer_next, moment_next = nesterov(outer_params[0], outer_momentum[0], own + came, 64)
    mine = outer_next.astype(jnp.bfloat16)
    theirs = lax.ppermute(mine, "zh", [(0, 1), (1, 0)])

    rows2 = put(put(rows, a, me - 3), b, me + 3)
    a, b = hop(a, b, 3)
    rows, t2, w3, theirs = hold((rows2, t2, w3, theirs))
    t1 = inward(jnp.concatenate([t2, rest]), 1)
    w3 = inward(w3, 2)
    pair = jnp.where(zh == 0, jnp.stack([mine, theirs]), jnp.stack([theirs, mine]))

    x = jnp.where(low, b, a)
    rows3 = put(rows, x, jnp.where(low, me + 4, me - 4))
    x = hop_out(x, 4)
    rows, t1, w3, w1, w2, pair = hold((rows3, t1, w3, w_rest, w_rest, pair))
    near = jnp.concatenate([t1, rest])
    far = lax.ppermute(near, "tensor", [(3, 4), (4, 3)])
    w13 = inward(jnp.concatenate([w1, w3]), 1)
    w2 = inward(w2, 2)

    rows4 = put(rows, x, jnp.where(low, me + 5, me - 5))
    x = hop_out(x, 5)
    rows, w2, w13, far = hold((rows4, w2, w13, far))
    w2 = inward(w2, 1)
    synced = lax.all_to_all(jnp.broadcast_to(pair[None], (32, 2, 16, 512)), PLANE, 0, 0, tiled=True)

    y = hop_out(x, 6)
    rows, w2, synced = hold((rows, w2, synced))
    rows = put(rows, x, jnp.where(low, me + 6, me - 6))
    mine3, back1, back3 = middle_products(low, near, far, w_rest, w13)
    (back2,) = middle_products(low, near, far, w2)
    back1, back2, back3 = [
        lax.ppermute(block, "tensor", [(3, 3 - d), (4, 4 + d)])
        for d, block in ((1, back1), (2, back2), (3, back3))
    ]
    synced = synced.transpose(1, 0, 2, 3).reshape(1024, 512)
    key_rows = last_step(me, weight, y, rows, mine3, back1, back2, back3, *rotary_tables(512))
    return (key_rows, outer_next[None], moment_next[None], synced[None])


def solution(mesh):
    fine = Mesh(mesh.devices.reshape(2, 4, 4, 2, 8), REPLICA + ("tensor",))
    in_specs = (
        P(REPLICA + ("tensor",), None),
        P(),
        P(REPLICA, None, "tensor"),
        P(REPLICA, "tensor", None, None),
        P("tensor", REPLICA, None),
        P("tensor", REPLICA, None),
    )
    out_specs = (
        P(REPLICA, "tensor"),
        P("tensor", REPLICA, None),
        P("tensor", REPLICA, None),
        P("tensor", None, None),
    )
    return jax.shard_map(body, mesh=fine, in_specs=in_specs, out_specs=out_specs, check_vma=False)
```
